32 devices in a mesh: depth: 2 (over core), row: 4 (over y, x), col: 4 (over z).
Axes of the slice: x: 2, y: 2, z: 4, core: 2. Of those that a mesh axis runs over, the one named last changes fastest.
Arguments:
- a_blocks: float32 [32, 8, 4096], P('row', 'col'), may hold values from -0.75 to 0.75
- a_index: int32 [32, 8], P('row', 'col'), may hold values from -1 to 1023, as said below
- b_blocks: float32 [64, 8, 4096], P('col', 'row'), may hold values from -6 to 6
- b_index: int32 [64, 8], P('col', 'row'), may hold values from -1 to 1023, as said below
- c_index: int32 [32, 16], P('row', 'col'), may hold values from -1 to 15, as said below
Outputs:
- c_blocks: float32 [32, 16, 4096], P('row', 'col')
The draws below stay inside these ranges and needn't reach their ends.
Inputs may be any that keep to these rules, and one draw needn't show every extreme that they name: `a_index`: slots j * 2 to (j + 1) * 2 - 1 of a block row hold block columns of k-panel j, that is j * 256 to (j + 1) * 256 - 1, or -1; the block columns of one row are distinct. Every slot group of some block rows is full. `b_index`: slots i * 2 to (i + 1) * 2 - 1 of a block column hold block rows i * 256 to (i + 1) * 256 - 1, or -1; the block rows of one column are distinct. Every slot group of some block columns is full. `c_index`: the kept block columns of one slot group of a row are distinct. Every slot group of some block rows is full.
All inputs are finite; a program needn't handle non-finite values.
Results may differ from the reference program's by a relative error of at most 0.0003.
Values sent between devices are 32-bit elements; how exact they have to be, the bound alone decides.
No kernel may reach another device: no remote copies, remote signals or barrier semaphores. Data moves between devices by JAX's collectives and lax.ppermute only.
A program may use at most 128 MiB of HBM per device.

```python
import jax
import jax.numpy as jnp
from jax import lax

BS = 64
KB = 1024
MB_DEV = 8
NW_DEV = 16
SA = 2
SB = 2
SC = 4
MB = 32
NW = 64
KP = 256
KQ = 256
N_ROW = 4
N_COL = 4


window_span = 8


def pick_distinct(key, pool, take_count):
    pool_width = pool.shape[-1]
    scores = jax.random.randint(key, pool.shape, 0, 1 << 20) * pool_width + jnp.arange(pool_width, dtype=jnp.int32)
    ranking = jnp.argsort(scores, axis=-1, stable=True)[..., :take_count]
    return jnp.take_along_axis(pool, ranking, axis=-1)


def live_mask(key, lead_rows, others, offset):
    threshold_draw = jax.random.randint(key, (lead_rows,) + others, 0, lead_rows)
    limits = (jnp.arange(lead_rows) + offset).reshape((lead_rows,) + (1,) * len(others))
    return threshold_draw < limits


def draw_a_index(key, part):
    panels = KB // KP
    rows = jnp.arange(MB, dtype=jnp.int32)
    centers = rows % MB_DEV * KP // MB_DEV
    offsets = jnp.arange(window_span, dtype=jnp.int32)
    where_in = (centers[:, None, None] - window_span // 2 + offsets[None, None, :]) % KP
    pool = where_in + (jnp.arange(panels, dtype=jnp.int32) * KP)[None, :, None]
    picked = pick_distinct(jax.random.fold_in(key, 21), pool, SA)
    is_live = live_mask(jax.random.fold_in(key, 22), MB, (panels, SA), MB // 3)
    return jnp.where(is_live, picked, -1).reshape(MB, panels * SA).astype(jnp.int32)


def draw_b_index(key, part):
    panels = KB // KQ
    inside = KQ // KP
    columns = jnp.arange(NW, dtype=jnp.int32)
    centers = columns % NW_DEV * KP // NW_DEV
    offsets = jnp.arange(window_span, dtype=jnp.int32)
    where_in = (centers[:, None, None, None] - window_span // 2 + offsets[None, None, None, :]) % KP
    bases = (jnp.arange(panels, dtype=jnp.int32)[:, None] * inside + jnp.arange(inside, dtype=jnp.int32)[None, :]) * KP
    pool = (where_in + bases[None, :, :, None]).reshape(NW, panels, inside * window_span)
    picked = pick_distinct(jax.random.fold_in(key, 31), pool, SB)
    is_live = live_mask(jax.random.fold_in(key, 32), NW, (panels, SB), NW // 3)
    return jnp.where(is_live, picked, -1).reshape(NW, panels * SB).astype(jnp.int32)


def draw_c_index(key, part):
    panels = NW // NW_DEV
    spread = min(SC + 2, NW_DEV)
    rows = jnp.arange(MB, dtype=jnp.int32)
    centers = rows % MB_DEV * NW_DEV // MB_DEV
    offsets = jnp.arange(spread, dtype=jnp.int32)
    near = (centers[:, None, None] - spread // 2 + offsets[None, None, :]) % NW_DEV
    pool = jnp.broadcast_to(near, (MB, panels, spread))
    picked = pick_distinct(jax.random.fold_in(key, 41), pool, SC)
    is_live = live_mask(jax.random.fold_in(key, 42), MB, (panels, SC), MB // 2)
    return jnp.where(is_live, picked, -1).reshape(MB, panels * SC).astype(jnp.int32)


def block_scale(stream_key, extent, cuts, smallest, top_value):
    def one(position, shards_of):
        draws = jax.random.uniform(jax.random.fold_in(jax.random.fold_in(stream_key, 6), position), (shards_of,), jnp.float32, smallest / len(cuts), top_value / len(cuts))
        return jnp.repeat(jnp.exp(draws), extent[position] // shards_of).reshape((-1,) + (1,) * (len(extent) - position - 1))

    loudness = one(*cuts[0])
    for cut in cuts[1:]:
        loudness = loudness * one(*cut)
    return loudness


def gaussian(stream_key, extent, width, reach, split=(), kind=jnp.bfloat16):
    array = width * jax.random.normal(stream_key, extent, jnp.float32)
    if split:
        array = array * block_scale(stream_key, extent, split, -0.22, 0.18)
    return jnp.clip(array, -reach, reach).astype(kind)


def setup_inputs(seed: int = 0) -> dict:
    arg_keys = jax.random.split(jax.random.key(seed), 6)
    return {
        "a_blocks": gaussian(arg_keys[0], (MB, N_COL * SA, BS * BS), BS ** -0.5, 0.75, ((0, 4), (1, 4)), jnp.float32),
        "a_index": draw_a_index(jax.random.fold_in(arg_keys[5], 71), 0),
        "b_blocks": gaussian(arg_keys[2], (NW, N_ROW * SB, BS * BS), 1.0, 6.0, ((0, 4), (1, 4)), jnp.float32),
        "b_index": draw_b_index(jax.random.fold_in(arg_keys[5], 71), 0),
        "c_index": draw_c_index(jax.random.fold_in(arg_keys[5], 71), 0),
    }


def reference(a_blocks, a_index, b_blocks, b_index, c_index):
    slots_b = b_index.shape[1]
    slots_a = a_index.shape[1]
    slots_c = c_index.shape[1]
    valid_b = b_index >= 0
    target = jnp.where(valid_b, b_index, KB).astype(jnp.int32)
    row_ids = jnp.broadcast_to(jnp.arange(NW, dtype=jnp.int32)[:, None], b_index.shape)
    slot_ids = jnp.broadcast_to(jnp.arange(slots_b, dtype=jnp.int32)[None, :], b_index.shape)
    pos_b = jnp.full((NW, KB + 1), -1, jnp.int32).at[row_ids, target].set(slot_ids)[:, :KB]
    b_four = b_blocks.reshape(NW, slots_b, BS, BS)
    group_ids = (jnp.arange(slots_c, dtype=jnp.int32) // SC).astype(jnp.int32)

    def one_row(packed):
        a_row, a_idx, c_idx = packed
        n_glob = jnp.where(c_idx >= 0, group_ids * NW_DEV + c_idx, 0).astype(jnp.int32)
        k_safe = jnp.where(a_idx >= 0, a_idx, 0).astype(jnp.int32)
        u_ids = pos_b[n_glob[:, None], k_safe[None, :]]
        usable = (c_idx >= 0)[:, None] & (a_idx >= 0)[None, :] & (u_ids >= 0)
        chosen = b_four[n_glob[:, None], jnp.where(usable, u_ids, 0).astype(jnp.int32)]
        chosen = jnp.where(usable[:, :, None, None], chosen, jnp.zeros((), chosen.dtype))
        a_four = a_row.reshape(slots_a, BS, BS)
        result = jnp.einsum("sac,tscx->tax", a_four, chosen, precision=lax.Precision.HIGHEST)
        return result.reshape(slots_c, BS * BS)

    return lax.map(one_row, (a_blocks, a_index, c_index))
```

```python
import functools

import jax
import jax.numpy as jnp
from jax import lax
from jax.experimental import pallas as pl
from jax.experimental.pallas import tpu as pltpu
from jax.sharding import PartitionSpec as P


BS = 64
LANES = 128
HALF = BS * BS // LANES
AXES = ("depth", "row", "col")
UNROLL = 2
VMEM = pl.BlockSpec(memory_space=pltpu.VMEM)
SMEM = pl.BlockSpec(memory_space=pltpu.SMEM)


def plan(n_row, n_col):
    half, n = n_row // 2, n_col // 2
    ratio = n_col // n_row
    place = lambda d, i, j: (d * n_row + i) * n_col + j
    chips = [(i, j) for i in range(n_row) for j in range(n_col)]
    b_steps = [
        [((d, i, j), (d, i ^ hop, j)) for d, hop in enumerate((k, half + k - 1)) for i, j in chips]
        for k in range(1, half)
    ]
    b_steps.append(
        [((0, i, j), (1, i ^ (n_row - 1), j)) for i, j in chips] + [((1, i, j), (0, i, j)) for i, j in chips]
    )
    a_steps = []
    for r in reversed(range(n)):
        step = []
        for i in range(n_row):
            kinds = [[], []]
            for p in range(n_col):
                kinds[int((p // ratio) ^ i >= half)].append(p)
            for q in range(n):
                for d in (0, 1):
                    here, there = kinds[d][q], kinds[1 - d][q ^ r]
                    if r:
                        step.append(((1 - d, i, here), (d, i, there)))
                        step.append(((d, i, here), (d, i, kinds[d][q ^ r])))
                    else:
                        step.append(((d, i, here), (d, i, there)))
                        step.append(((1 - d, i, here), (d, i, here)))
        a_steps.append(step)
    flat = lambda steps: [[(place(*s), place(*t)) for s, t in step] for step in steps]
    for step in flat(a_steps) + flat(b_steps):
        assert [sorted(x) for x in zip(*step)] == [list(range(2 * n_row * n_col))] * 2
    return flat(a_steps), flat(b_steps)


def rows_of(blocks):
    n, slots, _ = blocks.shape
    return blocks.reshape(n, slots, HALF, LANES).transpose(0, 2, 1, 3).reshape(n * HALF * slots, LANES)


def blocks_of(rows, n, slots):
    return rows.reshape(n, HALF, slots, LANES).transpose(0, 2, 1, 3).reshape(n, slots, HALF * LANES)


def pick(refs, which, row, stride):
    value = refs[0][pl.ds(row, HALF, stride=stride), :]
    for k in range(1, len(refs)):
        value = jnp.where(which == k, refs[k][pl.ds(row, HALF, stride=stride), :], value)
    return value


def packed(fields):
    code, shift = jnp.int32(0), 0
    for value, size in reversed(fields):
        code = code | (value << shift)
        shift += (size - 1).bit_length()
    return code


def unpacked(code, sizes):
    values = []
    for size in reversed(sizes):
        width = (size - 1).bit_length()
        values.append(code & ((1 << width) - 1))
        code = code >> width
    return values[::-1]


def list_kernel(dims, mesh_dims, c_ids, *refs):
    rows, cols, sa, sb, sc = dims
    n_row, n_col = mesh_dims
    n_a, n_b, ratio = n_col // 2, n_row // 2, n_col // n_row
    a_ids, b_ids = refs[:n_a], refs[n_a : n_a + n_b]
    total, entries, out = refs[n_a + n_b :]
    sizes = (rows, sc, cols, n_a, sa, n_b, sb)
    core, i, j = (lax.axis_index(name) for name in AXES)
    out[...] = jnp.zeros_like(out)
    count = jnp.int32(0)
    for x in range(n_b):
        q = i ^ jnp.where(core == 0, (x + 1) % n_b, n_b + x)
        for r in range(ratio):
            which = n_a - 1 - (((q * ratio + r) ^ j) & (n_a - 1))
            for m in range(rows):
                mine = []
                for s in range(sa):
                    k = a_ids[0][s, m]
                    for a in range(1, n_a):
                        k = jnp.where(which == a, a_ids[a][s, m], k)
                    mine.append(jnp.where(k < 0, -2, k))
                for t in range(sc):
                    n = c_ids[t, m]
                    at = jnp.maximum(n, 0)
                    for u in range(sb):
                        k = jnp.where(n < 0, -1, b_ids[x][u, at])
                        slot, hit = jnp.int32(0), k == mine[0]
                        for s in range(1, sa):
                            slot = jnp.where(k == mine[s], s, slot)
                            hit = hit | (k == mine[s])
                        entries[count] = packed(list(zip((m, t, at, which, slot, x, u), sizes)))
                        count = count + hit.astype(jnp.int32)
    for k in range(UNROLL):
        entries[count + k] = 0
    total[0] = count


def product_kernel(dims, n_a, n_b, total, entries, *refs):
    rows, cols, sa, sb, sc = dims
    a_refs, b_refs = refs[:n_a], refs[n_a : n_a + n_b]
    _, out, spread = refs[n_a + n_b :]
    sizes = (rows, sc, cols, n_a, sa, n_b, sb)
    count = total[0]
    low = lax.broadcasted_iota(jnp.int32, (HALF, LANES), 1) < BS

    def one(e, lane):
        m, t, c, a, s, b, u = unpacked(entries[e], sizes)
        x = pick(a_refs, a, m * (sa * HALF) + s, sa)
        x = jnp.where(e < count, x, 0.0)
        y = pick(b_refs, b, c * (sb * HALF) + u, sb)
        turned = pltpu.roll(y, BS, 1)
        wide = spread.at[lane]
        wide[pl.ds(0, HALF, stride=2), :] = jnp.where(low, y, 0.0)
        wide[pl.ds(1, HALF, stride=2), :] = jnp.where(low, turned, 0.0)
        wide[pl.ds(BS, HALF, stride=2), :] = jnp.where(low, 0.0, turned)
        wide[pl.ds(BS + 1, HALF, stride=2), :] = jnp.where(low, 0.0, y)
        w = wide[...]
        x_hi = x.astype(jnp.bfloat16)
        x_lo = (x - x_hi.astype(jnp.float32)).astype(jnp.bfloat16)
        w_hi = w.astype(jnp.bfloat16)
        w_lo = (w - w_hi.astype(jnp.float32)).astype(jnp.bfloat16)
        z = jnp.dot(
            jnp.concatenate([x_hi, x_lo], axis=0),
            jnp.concatenate([w_hi, w_lo], axis=1),
            preferred_element_type=jnp.float32,
        )
        z = (z[:HALF, :LANES] + z[HALF:, :LANES]) + (z[:HALF, LANES:] + z[HALF:, LANES:])
        return m * (sc * HALF) + t, z

    def step(k, carry):
        done = [one(k * UNROLL + lane, lane) for lane in range(UNROLL)]
        for row, z in done:
            where = (pl.ds(row, HALF, stride=sc), slice(None))
            out[where] = out[where] + z
        return carry

    lax.fori_loop(0, (count + UNROLL - 1) // UNROLL, step, 0)


def per_device(n_row, n_col, a_blocks, a_index, b_blocks, b_index, c_index):
    a_steps, b_steps = plan(n_row, n_col)
    dims = (a_index.shape[0], b_index.shape[0], a_index.shape[1], b_index.shape[1], c_index.shape[1])
    rows, _, sa, _, sc = dims
    full = jax.ShapeDtypeStruct((rows * HALF * sc, LANES), jnp.float32)
    cap = rows * sc * sa * (n_col // 2) + UNROLL + 6

    b_list = [rows_of(lax.ppermute(b_blocks, AXES, step)) for step in b_steps]
    a_list = [rows_of(lax.ppermute(a_blocks, AXES, step)) for step in a_steps]
    b_ids = [lax.ppermute(b_index.T, AXES, step) for step in b_steps]
    a_ids = [lax.ppermute(a_index.T, AXES, step) for step in a_steps]
    count, entries, empty = pl.pallas_call(
        functools.partial(list_kernel, dims, (n_row, n_col)),
        out_shape=[jax.ShapeDtypeStruct((1,), jnp.int32), jax.ShapeDtypeStruct((cap,), jnp.int32), full],
        in_specs=[SMEM] * (1 + len(a_ids) + len(b_ids)),
        out_specs=[SMEM, SMEM, VMEM],
        compiler_params=pltpu.CompilerParams(vmem_limit_bytes=16 * 1024 * 1024),
        cost_estimate=pl.CostEstimate(flops=0, bytes_accessed=1_000_000, transcendentals=0),
        name="list",
    )(c_index.T, *a_ids, *b_ids)
    part = pl.pallas_call(
        functools.partial(product_kernel, dims, len(a_list), len(b_list)),
        out_shape=full,
        in_specs=[SMEM] * 2 + [VMEM] * (len(a_list) + len(b_list) + 1),
        out_specs=VMEM,
        scratch_shapes=[pltpu.VMEM((UNROLL, LANES, LANES), jnp.float32)],
        input_output_aliases={2 + len(a_list) + len(b_list): 0},
        compiler_params=pltpu.CompilerParams(vmem_limit_bytes=16 * 1024 * 1024),
        cost_estimate=pl.CostEstimate(flops=100_000_000, bytes_accessed=2_000_000, transcendentals=0),
        name="products",
    )(count, entries, *a_list, *b_list, empty)
    other = lax.ppermute(part, "depth", [(0, 1), (1, 0)])
    return blocks_of(part + other, rows, sc)


def solution(mesh):
    placed = (
        P("row", "col", None),
        P("row", "col"),
        P("col", "row", None),
        P("col", "row"),
        P("row", "col"),
    )
    n_row, n_col = mesh.shape["row"], mesh.shape["col"]

    def body(*args):
        return per_device(n_row, n_col, *args)

    return jax.shard_map(
        body, mesh=mesh, in_specs=placed, out_specs=P("row", "col", None), check_vma=False
    )
```

```python
import functools

import jax
import jax.numpy as jnp
from jax import lax
from jax.experimental import pallas as pl
from jax.experimental.pallas import tpu as pltpu
from jax.sharding import PartitionSpec as P


BS = 64
LANES = 128
HALF = BS * BS // LANES
AXES = ("depth", "row", "col")
UNROLL = 2
VMEM = pl.BlockSpec(memory_space=pltpu.VMEM)
SMEM = pl.BlockSpec(memory_space=pltpu.SMEM)


def plan(n_row, n_col):
    half, n = n_row // 2, n_col // 2
    ratio = n_col // n_row
    place = lambda d, i, j: (d * n_row + i) * n_col + j
    chips = [(i, j) for i in range(n_row) for j in range(n_col)]
    b_steps = [
        [((d, i, j), (d, i ^ hop, j)) for d, hop in enumerate((k, half + k - 1)) for i, j in chips]
        for k in range(1, half)
    ]
    b_steps.append(
        [((0, i, j), (1, i ^ (n_row - 1), j)) for i, j in chips] + [((1, i, j), (0, i, j)) for i, j in chips]
    )
    b_marks = [
        [((1 - d, i, j), (d, i ^ hop, j)) for d, hop in enumerate((k, half + k - 1)) for i, j in chips]
        for k in range(1, half)
    ]
    b_marks.append([((d, i, j), (d, i ^ hop, j)) for d, hop in enumerate((half, n_row - 1)) for i, j in chips])
    a_steps = []
    for r in reversed(range(n)):
        step = []
        for i in range(n_row):
            kinds = [[], []]
            for p in range(n_col):
                kinds[int((p // ratio) ^ i >= half)].append(p)
            for q in range(n):
                for d in (0, 1):
                    here, there = kinds[d][q], kinds[1 - d][q ^ r]
                    if r:
                        step.append(((1 - d, i, here), (d, i, there)))
                        step.append(((d, i, here), (d, i, kinds[d][q ^ r])))
                    else:
                        step.append(((d, i, here), (d, i, there)))
                        step.append(((1 - d, i, here), (d, i, here)))
        a_steps.append(step)
    flat = lambda steps: [[(place(*s), place(*t)) for s, t in step] for step in steps]
    for step in flat(a_steps) + flat(b_steps) + flat(b_marks):
        assert [sorted(x) for x in zip(*step)] == [list(range(2 * n_row * n_col))] * 2
    return flat(a_steps), flat(b_steps), flat(b_marks)


def rows_of(blocks):
    n, slots, _ = blocks.shape
    return blocks.reshape(n, slots, HALF, LANES).transpose(0, 2, 1, 3).reshape(n * HALF * slots, LANES)


def blocks_of(rows, n, slots):
    return rows.reshape(n, HALF, slots, LANES).transpose(0, 2, 1, 3).reshape(n, slots, HALF * LANES)


def pick(refs, which, row, stride):
    value = refs[0][pl.ds(row, HALF, stride=stride), :]
    for k in range(1, len(refs)):
        value = jnp.where(which == k, refs[k][pl.ds(row, HALF, stride=stride), :], value)
    return value


def packed(fields):
    code, shift = jnp.int32(0), 0
    for value, size in reversed(fields):
        code = code | (value << shift)
        shift += (size - 1).bit_length()
    return code


def unpacked(code, sizes):
    values = []
    for size in reversed(sizes):
        width = (size - 1).bit_length()
        values.append(code & ((1 << width) - 1))
        code = code >> width
    return values[::-1]


def list_kernel(dims, mesh_dims, c_ids, *refs):
    rows, cols, sa, sb, sc = dims
    n_row, n_col = mesh_dims
    n_a, n_b, ratio = n_col // 2, n_row // 2, n_col // n_row
    a_ids, b_ids = refs[:n_a], refs[n_a : n_a + n_b]
    own, entries, out = refs[n_a + n_b :]
    sizes = (rows, sc, cols, n_a, sa, n_b, sb)
    core, i, j = (lax.axis_index(name) for name in AXES)
    out[...] = jnp.zeros_like(out)
    count = jnp.int32(1)
    for x in range(n_b):
        q = i ^ jnp.where(core == 0, (x + 1) % n_b, n_b + x)
        for r in range(ratio):
            which = n_a - 1 - (((q * ratio + r) ^ j) & (n_a - 1))
            for m in range(rows):
                mine = []
                for s in range(sa):
                    k = a_ids[0][s, m]
                    for a in range(1, n_a):
                        k = jnp.where(which == a, a_ids[a][s, m], k)
                    mine.append(jnp.where(k < 0, -2, k))
                for t in range(sc):
                    n = c_ids[t, m]
                    at = jnp.maximum(n, 0)
                    for u in range(sb):
                        k = b_ids[x][u, at]
                        if x == n_b - 1:
                            k = jnp.where(core == 0, own[u, at], k)
                        k = jnp.where(n < 0, -1, k)
                        slot, hit = jnp.int32(0), k == mine[0]
                        for s in range(1, sa):
                            slot = jnp.where(k == mine[s], s, slot)
                            hit = hit | (k == mine[s])
                        entries[count] = packed(list(zip((m, t, at, which, slot, x, u), sizes)))
                        count = count + hit.astype(jnp.int32)
    for k in range(UNROLL):
        entries[count + k] = 0
    entries[0] = count - 1


def product_kernel(dims, n_a, n_b, entries, *refs):
    rows, cols, sa, sb, sc = dims
    a_refs, b_refs = refs[:n_a], refs[n_a : n_a + n_b]
    _, out, spread = refs[n_a + n_b :]
    sizes = (rows, sc, cols, n_a, sa, n_b, sb)
    count = entries[0]
    low = lax.broadcasted_iota(jnp.int32, (HALF, LANES), 1) < BS

    def one(e, lane):
        m, t, c, a, s, b, u = unpacked(entries[1 + e], sizes)
        x = pick(a_refs, a, m * (sa * HALF) + s, sa)
        x = jnp.where(e < count, x, 0.0)
        y = pick(b_refs, b, c * (sb * HALF) + u, sb)
        turned = pltpu.roll(y, BS, 1)
        wide = spread.at[lane]
        wide[pl.ds(0, HALF, stride=2), :] = jnp.where(low, y, 0.0)
        wide[pl.ds(1, HALF, stride=2), :] = jnp.where(low, turned, 0.0)
        wide[pl.ds(BS, HALF, stride=2), :] = jnp.where(low, 0.0, turned)
        wide[pl.ds(BS + 1, HALF, stride=2), :] = jnp.where(low, 0.0, y)
        w = wide[...]
        x_hi = x.astype(jnp.bfloat16)
        x_lo = (x - x_hi.astype(jnp.float32)).astype(jnp.bfloat16)
        w_hi = w.astype(jnp.bfloat16)
        w_lo = (w - w_hi.astype(jnp.float32)).astype(jnp.bfloat16)
        z = jnp.dot(
            jnp.concatenate([x_hi, x_lo], axis=0),
            jnp.concatenate([w_hi, w_lo], axis=1),
            preferred_element_type=jnp.float32,
        )
        z = (z[:HALF, :LANES] + z[HALF:, :LANES]) + (z[:HALF, LANES:] + z[HALF:, LANES:])
        return m * (sc * HALF) + t, z

    def step(k, carry):
        done = [one(k * UNROLL + lane, lane) for lane in range(UNROLL)]
        for row, z in done:
            where = (pl.ds(row, HALF, stride=sc), slice(None))
            out[where] = out[where] + z
        return carry

    lax.fori_loop(0, (count + UNROLL - 1) // UNROLL, step, 0)


def per_device(n_row, n_col, a_blocks, a_index, b_blocks, b_index, c_index):
    a_steps, b_steps, b_marks = plan(n_row, n_col)
    dims = (a_index.shape[0], b_index.shape[0], a_index.shape[1], b_index.shape[1], c_index.shape[1])
    rows, _, sa, _, sc = dims
    full = jax.ShapeDtypeStruct((rows * HALF * sc, LANES), jnp.float32)
    cap = rows * sc * sa * (n_col // 2) + UNROLL + 6

    b_list = [rows_of(lax.ppermute(b_blocks, AXES, step)) for step in b_steps]
    a_list = [rows_of(lax.ppermute(a_blocks, AXES, step)) for step in a_steps]
    b_ids = [lax.ppermute(b_index.T, AXES, step) for step in b_marks]
    a_ids = [lax.ppermute(a_index.T, AXES, step) for step in a_steps]
    entries, empty = pl.pallas_call(
        functools.partial(list_kernel, dims, (n_row, n_col)),
        out_shape=[jax.ShapeDtypeStruct((cap,), jnp.int32), full],
        in_specs=[SMEM] * (2 + len(a_ids) + len(b_ids)),
        out_specs=[SMEM, VMEM],
        compiler_params=pltpu.CompilerParams(vmem_limit_bytes=16 * 1024 * 1024),
        cost_estimate=pl.CostEstimate(flops=0, bytes_accessed=1_000_000, transcendentals=0),
        name="list",
    )(c_index.T, *a_ids, *b_ids, b_index.T)
    part = pl.pallas_call(
        functools.partial(product_kernel, dims, len(a_list), len(b_list)),
        out_shape=full,
        in_specs=[SMEM] + [VMEM] * (len(a_list) + len(b_list) + 1),
        out_specs=VMEM,
        scratch_shapes=[pltpu.VMEM((UNROLL, LANES, LANES), jnp.float32)],
        input_output_aliases={1 + len(a_list) + len(b_list): 0},
        compiler_params=pltpu.CompilerParams(vmem_limit_bytes=16 * 1024 * 1024),
        cost_estimate=pl.CostEstimate(flops=100_000_000, bytes_accessed=2_000_000, transcendentals=0),
        name="products",
    )(entries, *a_list, *b_list, empty)
    other = lax.ppermute(part, "depth", [(0, 1), (1, 0)])
    return blocks_of(part + other, rows, sc)


def solution(mesh):
    placed = (
        P("row", "col", None),
        P("row", "col"),
        P("col", "row", None),
        P("col", "row"),
        P("row", "col"),
    )
    n_row, n_col = mesh.shape["row"], mesh.shape["col"]

    def body(*args):
        return per_device(n_row, n_col, *args)

    return jax.shard_map(
        body, mesh=mesh, in_specs=placed, out_specs=P("row", "col", None), check_vma=False
    )
```

```python
import functools

import jax
import jax.numpy as jnp
from jax import lax
from jax.experimental import pallas as pl
from jax.experimental.pallas import tpu as pltpu
from jax.sharding import PartitionSpec as P


BS = 64
LANES = 128
HALF = BS * BS // LANES
AXES = ("depth", "row", "col")
UNROLL = 4
VMEM = pl.BlockSpec(memory_space=pltpu.VMEM)
SMEM = pl.BlockSpec(memory_space=pltpu.SMEM)


def plan(n_row, n_col):
    half, n = n_row // 2, n_col // 2
    ratio = n_col // n_row
    place = lambda d, i, j: (d * n_row + i) * n_col + j
    chips = [(i, j) for i in range(n_row) for j in range(n_col)]
    b_steps = [
        [((d, i, j), (d, i ^ hop, j)) for d, hop in enumerate((k, half + k - 1)) for i, j in chips]
        for k in range(1, half)
    ]
    b_steps.append(
        [((0, i, j), (1, i ^ (n_row - 1), j)) for i, j in chips] + [((1, i, j), (0, i, j)) for i, j in chips]
    )
    b_marks = [
        [((1 - d, i, j), (d, i ^ hop, j)) for d, hop in enumerate((k, half + k - 1)) for i, j in chips]
        for k in range(1, half)
    ]
    b_marks.append([((d, i, j), (d, i ^ hop, j)) for d, hop in enumerate((half, n_row - 1)) for i, j in chips])
    a_steps = []
    for r in range(n):
        step = []
        for i in range(n_row):
            kinds = [[], []]
            for p in range(n_col):
                kinds[int((p // ratio) ^ i >= half)].append(p)
            for q in range(n):
                for d in (0, 1):
                    here, there = kinds[d][q], kinds[1 - d][q ^ r]
                    if r < n - 1:
                        step.append(((1 - d, i, here), (d, i, there)))
                        step.append(((d, i, here), (d, i, kinds[d][q ^ (r + 1)])))
                    else:
                        step.append(((d, i, here), (d, i, there)))
                        step.append(((1 - d, i, here), (d, i, here)))
        a_steps.append(step)
    flat = lambda steps: [[(place(*s), place(*t)) for s, t in step] for step in steps]
    for step in flat(a_steps) + flat(b_steps) + flat(b_marks):
        assert [sorted(x) for x in zip(*step)] == [list(range(2 * n_row * n_col))] * 2
    return flat(a_steps), flat(b_steps), flat(b_marks)


def rows_of(blocks):
    n, slots, _ = blocks.shape
    return blocks.reshape(n, slots, HALF, LANES).transpose(0, 2, 1, 3).reshape(n * HALF * slots, LANES)


def blocks_of(rows, n, slots):
    return rows.reshape(n, HALF, slots, LANES).transpose(0, 2, 1, 3).reshape(n, slots, HALF * LANES)


def pick(refs, which, row, stride):
    value = refs[0][pl.ds(row, HALF, stride=stride), :]
    for k in range(1, len(refs)):
        value = jnp.where(which == k, refs[k][pl.ds(row, HALF, stride=stride), :], value)
    return value


def packed(fields):
    code, shift = jnp.int32(0), 0
    for value, size in reversed(fields):
        code = code | (value << shift)
        shift += (size - 1).bit_length()
    return code


def unpacked(code, sizes):
    values = []
    for size in reversed(sizes):
        width = (size - 1).bit_length()
        values.append(code & ((1 << width) - 1))
        code = code >> width
    return values[::-1]


def list_kernel(dims, mesh_dims, c_ids, *refs):
    rows, cols, sa, sb, sc = dims
    n_row, n_col = mesh_dims
    n_a, n_b, ratio = n_col // 2, n_row // 2, n_col // n_row
    a_ids, b_ids = refs[:n_a], refs[n_a : n_a + n_b]
    own, entries, out = refs[n_a + n_b :]
    sizes = (rows, sc, cols, n_a, sa, n_b, sb)
    core, i, j = (lax.axis_index(name) for name in AXES)
    out[...] = jnp.zeros_like(out)
    panels = []
    for x in range(n_b):
        q = i ^ jnp.where(core == 0, (x + 1) % n_b, n_b + x)
        for r in range(ratio):
            apart = (q * ratio + r) ^ j
            which = jnp.where(apart & n_a != 0, apart, apart - 1) & (n_a - 1)
            panels.append((x, which, packed(list(zip((0, 0, 0, which, 0, x, 0), sizes)))))
    second = [packed(list(zip((0, 0, 0, 0, s, 0, 0), sizes))) for s in range(sa)]
    count = jnp.int32(1)
    for m in range(rows):
        mine = []
        for _, which, _ in panels:
            ks = []
            for s in range(sa):
                k = a_ids[0][s, m]
                for a in range(1, n_a):
                    k = jnp.where(which == a, a_ids[a][s, m], k)
                ks.append(jnp.where(k < 0, -2, k))
            mine.append(ks)
        for t in range(sc):
            n = c_ids[t, m]
            at = jnp.maximum(n, 0)
            base = packed(list(zip((m, t, at, 0, 0, 0, 0), sizes)))
            for (x, _, code), ks in zip(panels, mine):
                for u in range(sb):
                    k = b_ids[x][u, at]
                    if x == n_b - 1:
                        k = jnp.where(core == 0, own[u, at], k)
                    k = jnp.where(n < 0, -1, k)
                    slot, hit = jnp.int32(0), k == ks[0]
                    for s in range(1, sa):
                        slot = jnp.where(k == ks[s], second[s], slot)
                        hit = hit | (k == ks[s])
                    entries[count] = base + code + (slot + u)
                    count = count + hit.astype(jnp.int32)
    for k in range(UNROLL):
        entries[count + k] = 0
    entries[0] = count - 1


def product_kernel(dims, n_a, n_b, entries, *refs):
    rows, cols, sa, sb, sc = dims
    a_refs, b_refs = refs[:n_a], refs[n_a : n_a + n_b]
    _, out, spread = refs[n_a + n_b :]
    sizes = (rows, sc, cols, n_a, sa, n_b, sb)
    count = entries[0]
    low = lax.broadcasted_iota(jnp.int32, (HALF, LANES), 1) < BS

    def one(e, lane):
        m, t, c, a, s, b, u = unpacked(entries[1 + e], sizes)
        x = pick(a_refs, a, m * (sa * HALF) + s, sa)
        x = jnp.where(e < count, x, 0.0)
        y = pick(b_refs, b, c * (sb * HALF) + u, sb)
        turned = pltpu.roll(y, BS, 1)
        wide = spread.at[lane]
        wide[pl.ds(0, HALF, stride=2), :] = jnp.where(low, y, 0.0)
        wide[pl.ds(1, HALF, stride=2), :] = jnp.where(low, turned, 0.0)
        wide[pl.ds(BS, HALF, stride=2), :] = jnp.where(low, 0.0, turned)
        wide[pl.ds(BS + 1, HALF, stride=2), :] = jnp.where(low, 0.0, y)
        w = wide[...]
        x_hi = x.astype(jnp.bfloat16)
        x_lo = (x - x_hi.astype(jnp.float32)).astype(jnp.bfloat16)
        w_hi = w.astype(jnp.bfloat16)
        w_lo = (w - w_hi.astype(jnp.float32)).astype(jnp.bfloat16)
        z = jnp.dot(
            jnp.concatenate([x_hi, x_lo], axis=0),
            jnp.concatenate([w_hi, w_lo], axis=1),
            preferred_element_type=jnp.float32,
        )
        z = (z[:HALF, :LANES] + z[HALF:, :LANES]) + (z[:HALF, LANES:] + z[HALF:, LANES:])
        return m * (sc * HALF) + t, z

    def step(k, carry):
        done = [one(k * UNROLL + lane, lane) for lane in range(UNROLL)]
        for row, z in done:
            where = (pl.ds(row, HALF, stride=sc), slice(None))
            out[where] = out[where] + z
        return carry

    lax.fori_loop(0, (count + UNROLL - 1) // UNROLL, step, 0)


def per_device(n_row, n_col, a_blocks, a_index, b_blocks, b_index, c_index):
    a_steps, b_steps, b_marks = plan(n_row, n_col)
    dims = (a_index.shape[0], b_index.shape[0], a_index.shape[1], b_index.shape[1], c_index.shape[1])
    rows, _, sa, _, sc = dims
    full = jax.ShapeDtypeStruct((rows * HALF * sc, LANES), jnp.float32)
    cap = rows * sc * sa * (n_col // 2) + UNROLL + 6

    b_list = [rows_of(lax.ppermute(b_blocks, AXES, step)) for step in b_steps]
    a_list = [rows_of(lax.ppermute(a_blocks, AXES, step)) for step in a_steps]
    b_ids = [lax.ppermute(b_index.T, AXES, step) for step in b_marks]
    a_ids = [lax.ppermute(a_index.T, AXES, step) for step in a_steps]
    entries, empty = pl.pallas_call(
        functools.partial(list_kernel, dims, (n_row, n_col)),
        out_shape=[jax.ShapeDtypeStruct((cap,), jnp.int32), full],
        in_specs=[SMEM] * (2 + len(a_ids) + len(b_ids)),
        out_specs=[SMEM, VMEM],
        compiler_params=pltpu.CompilerParams(vmem_limit_bytes=16 * 1024 * 1024),
        cost_estimate=pl.CostEstimate(flops=0, bytes_accessed=1_000_000, transcendentals=0),
        name="list",
    )(c_index.T, *a_ids, *b_ids, b_index.T)
    part = pl.pallas_call(
        functools.partial(product_kernel, dims, len(a_list), len(b_list)),
        out_shape=full,
        in_specs=[SMEM] + [VMEM] * (len(a_list) + len(b_list) + 1),
        out_specs=VMEM,
        scratch_shapes=[pltpu.VMEM((UNROLL, LANES, LANES), jnp.float32)],
        input_output_aliases={1 + len(a_list) + len(b_list): 0},
        compiler_params=pltpu.CompilerParams(vmem_limit_bytes=16 * 1024 * 1024),
        cost_estimate=pl.CostEstimate(flops=100_000_000, bytes_accessed=2_000_000, transcendentals=0),
        name="products",
    )(entries, *a_list, *b_list, empty)
    other = lax.ppermute(part, "depth", [(0, 1), (1, 0)])
    return blocks_of(part + other, rows, sc)


def solution(mesh):
    placed = (
        P("row", "col", None),
        P("row", "col"),
        P("col", "row", None),
        P("col", "row"),
        P("row", "col"),
    )
    n_row, n_col = mesh.shape["row"], mesh.shape["col"]

    def body(*args):
        return per_device(n_row, n_col, *args)

    return jax.shard_map(
        body, mesh=mesh, in_specs=placed, out_specs=P("row", "col", None), check_vma=False
    )
```
